32 devices in a mesh: grp: 2 (over y), row: 4 (over z), col: 2 (over x), sub: 2 (over core).
Axes of the slice: x: 2, y: 2, z: 4, core: 2. Of those that a mesh axis runs over, the one named last changes fastest.
Arguments:
- recordings: float32 [4, 4096, 2000], P('grp', ('row', 'col'), 'sub'), parts along dimension 0, may hold values from -640 to 640
- filter_taps: float32 [129], replicated, may hold values from -0.5 to 0.5
- slot_table: int32 [4, 1024], P('row'), may hold values from 0 to 1023, each once within a row
- lag_count: int32 [4096], replicated, may hold values from 1 to 17
Outputs:
- xcorr: bfloat16 [34, 4096, 2, 2048], P('grp', ('row', 'sub'), 'col'), parts along dimension 0
The draws below stay inside these ranges and needn't reach their ends.
There are 2 independent parts, one for each index of `grp`. The reference program is written for one: setup_inputs(seed, part) draws one part's arguments, and reference() takes and returns one part's arrays. A program takes and returns all parts, laid end to end along the dimension named above; an argument that names none is the same for every part. Nothing has to cross between parts.
Inputs may be any that keep to these rules, and one draw needn't show every extreme that they name: Each row of slot_table names every slot of the block exactly once.
All inputs are finite; a program needn't handle non-finite values.
Results may differ from the reference program's by a relative error of at most 0.0052.
Values may be sent and summed in bfloat16 or wider, within the bound.
A program may use at most 192 MiB of HBM per device.

```python
import math
import jax
import jax.numpy as jnp
from jax import lax

C = 4096
SEGS = 2
TAPS = 129
LAGS = 17
TIME = 2000
TD = 1000
BLOCK = 1024
SPAN = 512
N_ROW = 4
N_COL = 2


def draw_recordings(key, part):
    key_scale, key_noise = jax.random.split(key, 2)
    channel_scale = jnp.exp(jax.random.uniform(key_scale, (SEGS, C, 1), jnp.float32, 0.0, math.log(10.0)))
    position = jnp.arange(TIME, dtype=jnp.float32) / TIME
    envelope = jnp.exp(position * math.log(10.0))
    base = jnp.clip(jax.random.normal(key_noise, (SEGS, C, TIME), jnp.float32), -4.0, 4.0)
    return (channel_scale * envelope * base).astype(jnp.float32)


def with_ends(drawn, rng, least, largest):
    longest = drawn.shape.index(max(drawn.shape))
    spots = []
    for shift in (0, 1):
        where = [jax.random.randint(jax.random.fold_in(rng, axis), (), 0, length) for axis, length in enumerate(drawn.shape)]
        where[longest] = (where[longest] + shift) % drawn.shape[longest]
        spots.append(tuple(where))
    return drawn.at[spots[0]].set(least).at[spots[1]].set(largest)


def scatter_about(rng, dims, spread, reach, held_as=jnp.bfloat16):
    return jnp.clip(spread * jax.random.normal(rng, dims, jnp.float32), -reach, reach).astype(held_as)


def setup_inputs(seed: int = 0, part: int = 0) -> dict:
    splits = jax.random.split(jax.random.key(seed), 5)
    own_keys = jax.random.split(jax.random.fold_in(splits[4], part), 5)
    recordings = draw_recordings(jax.random.fold_in(jax.random.fold_in(splits[4], part), 71), part)
    filter_taps = scatter_about(splits[1], (TAPS,), TAPS ** -0.5, 0.5, jnp.float32)
    slot_table = jax.vmap(lambda own: jax.random.permutation(own, BLOCK))(jax.random.split(splits[2], N_ROW)).reshape((N_ROW, BLOCK)).astype(jnp.int32)
    lag_count = with_ends(jax.random.randint(splits[3], (C,), 1, LAGS + 1), jax.random.fold_in(splits[3], 1), 1, LAGS).astype(jnp.int32)
    return {"recordings": recordings, "filter_taps": filter_taps, "slot_table": slot_table, "lag_count": lag_count}


stability = 1e-05

def reference(recordings, filter_taps, slot_table, lag_count):
    margin = (TAPS - 1) // 2
    padded = jnp.pad(recordings, ((0, 0), (0, 0), (margin, margin)))
    extent = padded.shape[2]
    filtered = lax.conv_general_dilated(padded.reshape(SEGS * C, 1, extent), filter_taps.reshape(1, 1, TAPS), (2,), 'VALID', precision=lax.Precision.HIGHEST).reshape(SEGS, C, TD)
    energy = lax.optimization_barrier(jnp.mean(filtered * filtered, axis=2, keepdims=True))
    whitened = (filtered * lax.rsqrt(energy + stability)).astype(jnp.bfloat16)
    chosen = (jnp.arange(N_ROW, dtype=jnp.int32)[:, None] * BLOCK + slot_table.astype(jnp.int32)).reshape(C)
    row_data = jnp.take(whitened, chosen, axis=1).astype(jnp.float32)
    column_data = whitened.reshape(SEGS, N_ROW, N_COL, SPAN, TD).transpose(0, 2, 1, 3, 4).reshape(SEGS, N_COL, N_ROW * SPAN, TD).astype(jnp.float32)
    lag_limits = lag_count.reshape(N_ROW, N_COL, SPAN).transpose(1, 0, 2).reshape(N_COL, N_ROW * SPAN)
    padded_cols = jnp.pad(column_data, ((0, 0), (0, 0), (0, 0), (0, LAGS)))
    factor = 1.0 / math.sqrt(SEGS * TD)

    def single_lag(lag_index):
        shifted = lax.dynamic_slice_in_dim(padded_cols, lag_index, TD, 3)
        product = jnp.einsum('sat,sqrt->aqr', row_data, shifted, precision=lax.Precision.HIGHEST)
        return jnp.where(lag_index < lag_limits[None], product * factor, 0.0).astype(jnp.bfloat16)
    return lax.map(single_lag, jnp.arange(LAGS, dtype=jnp.int32))
```

```python
import functools
import math

import jax
import jax.numpy as jnp
from jax import lax
from jax.experimental import pallas as pl
from jax.experimental.pallas import tpu as pltpu
from jax.sharding import PartitionSpec as P

LAGS = 17
PHASES = 8
SLOTS = 128
STABILITY = 1e-05


def nt_dot(a, b):
    return lax.dot_general(a, b, (((1,), (1,)), ((), ())), preferred_element_type=jnp.float32)


def nn_dot(a, b):
    return jnp.dot(a, b, preferred_element_type=jnp.float32)


def filter_kernel(samples, side_ref, own_ref, other_ref, taps_ref, out_ref, line, filtered):
    margin = 64
    width = own_ref.shape[1]
    window = 3 * 128
    order = lax.broadcasted_iota(jnp.int32, (128, window), 0)
    place = PHASES * (order % 16) + order // 16
    band = jnp.broadcast_to(taps_ref[...], (128, window))
    for bit in range(7):
        moved = pltpu.roll(band, 2 << bit, 1)
        band = jnp.where((place >> bit) & 1 == 1, moved, band)
    band_high = band.astype(jnp.bfloat16)
    band_low = (band - band_high.astype(jnp.float32)).astype(jnp.bfloat16)

    line[...] = jnp.zeros_like(line)

    @pl.when(side_ref[0] == 0)
    def _():
        line[margin : margin + width] = own_ref[0]
        line[margin + width : margin + 2 * width] = other_ref[0]

    @pl.when(side_ref[0] != 0)
    def _():
        line[margin : margin + width] = other_ref[0]
        line[margin + width : margin + 2 * width] = own_ref[0]

    tiles = SLOTS // 16
    row = lax.broadcasted_iota(jnp.int32, (128, 1), 0)
    energy = jnp.zeros((1, line.shape[1]), jnp.float32)
    for tile in range(tiles):
        part = line[256 * tile : 256 * tile + window]
        high = part.astype(jnp.bfloat16)
        low = (part - high.astype(jnp.float32)).astype(jnp.bfloat16)
        value = nn_dot(band_high, high) + (nn_dot(band_high, low) + nn_dot(band_low, high))
        index = PHASES * (16 * tile + row % 16) + row // 16
        value = jnp.where(index < samples, value, 0.0)
        energy = energy + jnp.sum(value * value, axis=0, keepdims=True)
        filtered[tile] = value
    scale = lax.rsqrt(energy / samples + STABILITY)
    for tile in range(tiles):
        value = (filtered[tile] * scale).astype(jnp.bfloat16)
        for phase in range(PHASES):
            out_ref[phase, 0, 16 * tile : 16 * tile + 16, :] = value[16 * phase : 16 * phase + 16]


def whiten(recordings, other, taps, side):
    segments, width, channels = recordings.shape
    half = channels // 2
    block = min(128, half)
    steps = half // block
    samples = width
    own_steps = steps
    if block % 128:
        recordings = lax.dynamic_slice_in_dim(recordings, side[0] * half, half, 2)
        own_steps = 0
    taps_row = jnp.pad(taps.reshape(1, -1), ((0, 0), (0, 384 - taps.shape[0])))
    out = pl.pallas_call(
        functools.partial(filter_kernel, samples),
        out_shape=jax.ShapeDtypeStruct((PHASES, segments, SLOTS, half), jnp.bfloat16),
        grid_spec=pltpu.PrefetchScalarGridSpec(
            num_scalar_prefetch=1,
            grid=(segments, steps),
            in_specs=[
                pl.BlockSpec((1, width, block), lambda s, c, side: (s, 0, side[0] * own_steps + c)),
                pl.BlockSpec((1, width, block), lambda s, c, side: (s, 0, c)),
                pl.BlockSpec((1, 384), lambda s, c, side: (0, 0)),
            ],
            out_specs=pl.BlockSpec((PHASES, 1, SLOTS, block), lambda s, c, side: (0, s, 0, c)),
            scratch_shapes=[
                pltpu.VMEM((256 * (SLOTS // 16 - 1) + 384, block), jnp.float32),
                pltpu.VMEM((SLOTS // 16, 128, block), jnp.float32),
            ],
        ),
        compiler_params=pltpu.CompilerParams(vmem_limit_bytes=16 << 20),
        name="whiten",
    )(side, recordings, other, taps_row)
    return out.reshape(PHASES * segments * SLOTS, half)


def rows_kernel(count, base_ref, slots_ref, *refs):
    pieces, out_ref = refs[:count], refs[count]
    phase = pl.program_id(0)
    rows = slots_ref.shape[0]
    total = None
    for k, piece in enumerate(pieces):
        width = piece.shape[1]
        channel = lax.broadcasted_iota(jnp.int32, (rows, width), 1) + base_ref[k]
        pick = (slots_ref[...] == channel).astype(jnp.float32).astype(jnp.bfloat16)
        term = nt_dot(pick, piece[...])
        total = term if total is None else total + term
    depth = total.shape[1]
    for carry in range(3):
        if carry:
            moved = jnp.concatenate(
                [
                    pltpu.roll(total[:, s : s + SLOTS], carry, 1)
                    for s in range(0, depth, SLOTS)
                ],
                axis=1,
            )
        else:
            moved = total
        start = pl.multiple_of((2 - carry) * PHASES * depth + phase * depth, depth)
        out_ref[:, pl.ds(start, depth)] = moved.astype(jnp.bfloat16)


def build_rows(slots, pieces, bases):
    rows = slots.shape[0]
    depth = pieces[0].shape[0] // PHASES
    return pl.pallas_call(
        functools.partial(rows_kernel, len(pieces)),
        out_shape=jax.ShapeDtypeStruct((rows, 3 * PHASES * depth), jnp.bfloat16),
        grid_spec=pltpu.PrefetchScalarGridSpec(
            num_scalar_prefetch=1,
            grid=(PHASES,),
            in_specs=[pl.BlockSpec((rows, 1), lambda j, base: (0, 0))]
            + [pl.BlockSpec((depth, p.shape[1]), lambda j, base: (j, 0)) for p in pieces],
            out_specs=pl.BlockSpec((rows, 3 * PHASES * depth), lambda j, base: (0, 0)),
        ),
        compiler_params=pltpu.CompilerParams(vmem_limit_bytes=24 << 20),
        name="rows",
    )(bases, slots, *pieces)


def correlate_kernel(factor, count, choices, depth, where_ref, rows_ref, limit_ref, *refs):
    pieces, out_ref, held, done = refs[: count * choices], refs[-3], refs[-2], refs[-1]
    lag = pl.program_id(0)
    length = PHASES * depth

    @pl.when(lag == 0)
    def _():
        for choice in range(choices):

            @pl.when(where_ref[3] == choice)
            def _():
                copies = [
                    pltpu.make_async_copy(pieces[count * choice + k], held.at[k], done.at[k])
                    for k in range(count)
                ]
                for copy in copies:
                    copy.start()
                for copy in copies:
                    copy.wait()

    start = pl.multiple_of((LAGS - 1 - lag) * depth, depth)
    rows = rows_ref[:, pl.ds(start, length)]
    width = held.shape[2]
    block = min(width, 256)
    for k in range(count):
        for first in range(0, width, block):
            spot = first
            if count > 1:
                spot = pl.multiple_of(where_ref[1 + k] * width + first, block)
            product = jnp.dot(
                rows, held[k, :, first : first + block], preferred_element_type=jnp.float32
            )
            keep = lag < limit_ref[:, pl.ds(spot, block)]
            out_ref[0, :, pl.ds(spot, block)] = jnp.where(keep, product * factor, 0.0).astype(
                jnp.bfloat16
            )


def correlate(rows, pieces, limits, where, factor, buffer):
    choices, count = len(pieces), len(pieces[0])
    depth = rows.shape[1] // (3 * PHASES)
    length = PHASES * depth
    portion = rows.shape[0]
    columns = limits.shape[1]
    run = pieces[0][0].shape[1]
    across = count * run
    pieces = [piece for group in pieces for piece in group]
    operands = [where, rows, limits, *pieces]
    in_specs = [
        pl.BlockSpec(rows.shape, lambda l, where: (0, 0), pipeline_mode=pl.Buffered(1)),
        pl.BlockSpec((1, across), lambda l, where: (0, where[0])),
    ] + [pl.BlockSpec(memory_space=pl.ANY) for _ in pieces]
    aliases = {}
    if buffer is not None:
        aliases = {len(operands): 0}
        operands.append(buffer)
        in_specs.append(pl.BlockSpec(memory_space=pl.ANY))
    work = LAGS * portion * across
    return pl.pallas_call(
        functools.partial(correlate_kernel, factor, count, choices, depth),
        out_shape=jax.ShapeDtypeStruct((LAGS, portion, columns), jnp.bfloat16),
        grid_spec=pltpu.PrefetchScalarGridSpec(
            num_scalar_prefetch=1,
            grid=(LAGS,),
            in_specs=in_specs,
            out_specs=pl.BlockSpec((1, portion, across), lambda l, where: (l, 0, where[0])),
            scratch_shapes=[
                pltpu.VMEM((count, length, run), jnp.bfloat16),
                pltpu.SemaphoreType.DMA((count,)),
            ],
        ),
        input_output_aliases=aliases,
        compiler_params=pltpu.CompilerParams(vmem_limit_bytes=20 << 20),
        cost_estimate=pl.CostEstimate(
            flops=2 * work * length,
            bytes_accessed=2 * (work + rows.size + length * across),
            transcendentals=0,
        ),
        name="correlate",
    )(*operands)


def swap(value, axis):
    return lax.ppermute(value, axis, [(0, 1), (1, 0)])


def shards(recordings, filter_taps, slot_table, lag_count):
    segments, channels, width = recordings.shape
    half = channels // 2
    side = lax.axis_index("sub")
    spot = lax.axis_index("row")
    across = lax.axis_index("col")
    row_count = lax.axis_size("row")
    col_count = lax.axis_size("col")
    portion = slot_table.shape[1] // 2
    factor = 1.0 / math.sqrt(segments * width)

    by_time = recordings.transpose(0, 2, 1)
    away = lax.dynamic_slice_in_dim(by_time, (1 - side) * half, half, 2)
    other = swap(away, "sub")
    mine = whiten(by_time, other, filter_taps, side.reshape(1))

    slots = lax.dynamic_slice_in_dim(slot_table[0], side * portion, portion).reshape(portion, 1)
    limits = lax.dynamic_slice_in_dim(
        lag_count.reshape(row_count, col_count, channels), across, 1, 1
    ).reshape(1, -1)

    if half % 128 or col_count != 2:
        whole = lax.all_gather(mine, "sub", axis=1, tiled=True)
        block = lax.all_gather(whole, "col", axis=1, tiled=True)
        rows = build_rows(slots, [block], jnp.zeros((1,), jnp.int32))
        columns = lax.all_gather(whole, "row", axis=1, tiled=True)
        start = jnp.zeros((4,), jnp.int32)
        result = correlate(rows, [[columns]], limits, start, factor, None)
        return result.reshape(LAGS, portion, 1, -1)

    rightward = [(i, i + 1) for i in range(row_count - 1)]
    leftward = [(i + 1, i) for i in range(row_count - 1)]

    def step(left, right):
        return lax.ppermute(left, "row", rightward), lax.ppermute(right, "row", leftward)

    mate = swap(mine, "sub")
    beside = swap(mine, "col")
    arrived = step(mine, mine)
    beside_mate = swap(beside, "sub")
    near, far = across * channels, (1 - across) * channels
    this, that = side * half, (1 - side) * half
    bases = jnp.stack([near + this, near + that, far + this, far + that]).astype(jnp.int32)
    beside, beside_mate, *arrived = lax.optimization_barrier((beside, beside_mate, *arrived))
    lefts, rights = [mine, arrived[0]], [mine, arrived[1]]
    rows = build_rows(slots, [mine, mate, beside, beside_mate], bases)

    def place(source, choice):
        return jnp.stack([source, side, 1 - side, choice]).astype(jnp.int32)

    orders = []
    for z in range(row_count):
        order = []
        for distance in range(1, row_count):
            ends = [(distance, 1), (distance, -1)]
            order += [(d, sign) for d, sign in ends if 0 <= z + sign * d < row_count]
        orders.append(order)

    mates = {}

    def choose(turn):
        kinds = sorted({orders[z][turn] for z in range(row_count)})
        pieces = []
        for distance, sign in kinds:
            piece = (rights if sign > 0 else lefts)[distance]
            if (distance, sign) not in mates:
                mates[distance, sign] = swap(piece, "sub")
            pieces.append([piece, mates[distance, sign]])
        source = choice = jnp.int32(0)
        for z in range(row_count):
            distance, sign = orders[z][turn]
            source = jnp.where(spot == z, z + sign * distance, source)
            choice = jnp.where(spot == z, kinds.index((distance, sign)), choice)
        return pieces, place(source, choice)

    result = None
    group, where = [[mine, mate]], place(spot, jnp.int32(0))
    for turn in range(row_count):
        last = turn == row_count - 1
        ahead = turn + 2 <= row_count - 1
        if ahead:
            arrived = step(lefts[-1], rights[-1])
        if not last:
            following = choose(turn)
        result = correlate(rows, group, limits, where, factor, result)
        if ahead:
            result, *arrived = lax.optimization_barrier((result, *arrived))
            lefts.append(arrived[0])
            rights.append(arrived[1])
        if not last:
            group, where = following
    return result.reshape(LAGS, portion, 1, -1)


def solution(mesh):
    return jax.shard_map(
        shards,
        mesh=mesh,
        in_specs=(P("grp", ("row", "col"), "sub"), P(), P("row", None), P()),
        out_specs=P("grp", ("row", "sub"), "col", None),
        check_vma=False,
    )
```

```python
import functools
import math

import jax
import jax.numpy as jnp
from jax import lax
from jax.experimental import pallas as pl
from jax.experimental.pallas import tpu as pltpu
from jax.sharding import PartitionSpec as P

LAGS = 17
PHASES = 8
SLOTS = 128
STABILITY = 1e-05


def nt_dot(a, b):
    return lax.dot_general(a, b, (((1,), (1,)), ((), ())), preferred_element_type=jnp.float32)


def nn_dot(a, b):
    return jnp.dot(a, b, preferred_element_type=jnp.float32)


def filter_kernel(samples, side_ref, own_ref, other_ref, taps_ref, out_ref, line, filtered):
    margin = 64
    width = own_ref.shape[1]
    window = 3 * 128
    order = lax.broadcasted_iota(jnp.int32, (128, window), 0)
    place = PHASES * (order % 16) + order // 16
    band = jnp.broadcast_to(taps_ref[...], (128, window))
    for bit in range(7):
        moved = pltpu.roll(band, 2 << bit, 1)
        band = jnp.where((place >> bit) & 1 == 1, moved, band)
    band_high = band.astype(jnp.bfloat16)
    band_low = (band - band_high.astype(jnp.float32)).astype(jnp.bfloat16)

    line[...] = jnp.zeros_like(line)

    @pl.when(side_ref[0] == 0)
    def _():
        line[margin : margin + width] = own_ref[0]
        line[margin + width : margin + 2 * width] = other_ref[0]

    @pl.when(side_ref[0] != 0)
    def _():
        line[margin : margin + width] = other_ref[0]
        line[margin + width : margin + 2 * width] = own_ref[0]

    tiles = SLOTS // 16
    row = lax.broadcasted_iota(jnp.int32, (128, 1), 0)
    energy = jnp.zeros((1, line.shape[1]), jnp.float32)
    for tile in range(tiles):
        part = line[256 * tile : 256 * tile + window]
        high = part.astype(jnp.bfloat16)
        low = (part - high.astype(jnp.float32)).astype(jnp.bfloat16)
        value = nn_dot(band_high, high) + (nn_dot(band_high, low) + nn_dot(band_low, high))
        index = PHASES * (16 * tile + row % 16) + row // 16
        value = jnp.where(index < samples, value, 0.0)
        energy = energy + jnp.sum(value * value, axis=0, keepdims=True)
        filtered[tile] = value
    scale = lax.rsqrt(energy / samples + STABILITY)
    for tile in range(tiles):
        value = (filtered[tile] * scale).astype(jnp.bfloat16)
        for phase in range(PHASES):
            out_ref[phase, 0, 16 * tile : 16 * tile + 16, :] = value[16 * phase : 16 * phase + 16]


def whiten(recordings, other, taps, side):
    segments, width, channels = recordings.shape
    half = channels // 2
    block = min(128, half)
    steps = half // block
    samples = width
    own_steps = steps
    if block % 128:
        recordings = lax.dynamic_slice_in_dim(recordings, side[0] * half, half, 2)
        own_steps = 0
    taps_row = jnp.pad(taps.reshape(1, -1), ((0, 0), (0, 384 - taps.shape[0])))
    out = pl.pallas_call(
        functools.partial(filter_kernel, samples),
        out_shape=jax.ShapeDtypeStruct((PHASES, segments, SLOTS, half), jnp.bfloat16),
        grid_spec=pltpu.PrefetchScalarGridSpec(
            num_scalar_prefetch=1,
            grid=(segments, steps),
            in_specs=[
                pl.BlockSpec((1, width, block), lambda s, c, side: (s, 0, side[0] * own_steps + c)),
                pl.BlockSpec((1, width, block), lambda s, c, side: (s, 0, c)),
                pl.BlockSpec((1, 384), lambda s, c, side: (0, 0)),
            ],
            out_specs=pl.BlockSpec((PHASES, 1, SLOTS, block), lambda s, c, side: (0, s, 0, c)),
            scratch_shapes=[
                pltpu.VMEM((256 * (SLOTS // 16 - 1) + 384, block), jnp.float32),
                pltpu.VMEM((SLOTS // 16, 128, block), jnp.float32),
            ],
        ),
        compiler_params=pltpu.CompilerParams(vmem_limit_bytes=16 << 20),
        name="whiten",
    )(side, recordings, other, taps_row)
    return out.reshape(PHASES * segments * SLOTS, half)


def row_blocks():
    blocks = [[(j, 1)] for j in range(PHASES)]

    def minus(a, b):
        return a + [(index, -sign) for index, sign in b]

    def outer(kind, k):
        even, odd, after = [(1 + 2 * k, 1)], [(2 + 2 * k, 1)], [(3 + 2 * k, 1)]
        return [minus(even, odd), odd, minus(after, odd)][kind]

    blocks += [outer(1, k) for k in range(PHASES + 3)]
    for first in (0, 2):
        for second in range(3):
            for k in range(5):
                even, odd = outer(first, 2 * k), outer(first, 2 * k + 1)
                if second == 0:
                    blocks.append(minus(even, odd))
                elif second == 1:
                    blocks.append(odd)
                else:
                    blocks.append(minus(outer(first, 2 * k + 2), odd))
    return blocks


def column_blocks():
    blocks = [[2 * k, 2 * k + 1] for k in range(4)]
    for first in (0, 1):
        for second in ([0], [0, 2], [2]):
            blocks += [[4 * k + first + b for b in second] for k in range(2)]
    return blocks


ROW_BLOCKS = PHASES + PHASES + 3 + 30
COLUMN_BLOCKS = 16


def rows_kernel(count, base_ref, slots_ref, *refs):
    pieces, out_ref, pick, shifted = refs[:count], refs[count], refs[count + 1], refs[count + 2]
    phase = pl.program_id(0)
    rows = slots_ref.shape[0]
    depth = pieces[0].shape[0]

    @pl.when(phase == 0)
    def _():
        first = 0
        for k, piece in enumerate(pieces):
            width = piece.shape[1]
            channel = lax.broadcasted_iota(jnp.int32, (rows, width), 1) + base_ref[k]
            chosen = (slots_ref[...] == channel).astype(jnp.float32).astype(jnp.bfloat16)
            pick[:, first : first + width] = chosen
            first += width

    total = None
    first = 0
    for piece in pieces:
        width = piece.shape[1]
        term = nt_dot(pick[:, first : first + width], piece[...])
        first += width
        total = term if total is None else total + term
    for carry in range(3):
        moved = total
        if carry:
            moved = jnp.concatenate(
                [
                    pltpu.roll(total[:, s : s + SLOTS], carry, 1)
                    for s in range(0, depth, SLOTS)
                ],
                axis=1,
            )
        shifted[(2 - carry) * PHASES + phase] = moved.astype(jnp.bfloat16)

    @pl.when(phase == PHASES - 1)
    def _():
        def block(terms):
            if len(terms) == 1:
                return shifted[terms[0][0]]
            value = None
            for index, sign in terms:
                part = shifted[index].astype(jnp.float32) * sign
                value = part if value is None else value + part
            return value.astype(jnp.bfloat16)

        for slot, terms in enumerate(row_blocks()):
            out_ref[:, slot * depth : (slot + 1) * depth] = block(terms)


def build_rows(slots, pieces, bases):
    rows = slots.shape[0]
    depth = pieces[0].shape[0] // PHASES
    return pl.pallas_call(
        functools.partial(rows_kernel, len(pieces)),
        out_shape=jax.ShapeDtypeStruct((rows, ROW_BLOCKS * depth), jnp.bfloat16),
        grid_spec=pltpu.PrefetchScalarGridSpec(
            num_scalar_prefetch=1,
            grid=(PHASES,),
            in_specs=[pl.BlockSpec((rows, 1), lambda j, base: (0, 0))]
            + [pl.BlockSpec((depth, p.shape[1]), lambda j, base: (j, 0)) for p in pieces],
            out_specs=pl.BlockSpec(
                (rows, ROW_BLOCKS * depth), lambda j, base: (0, 0), pipeline_mode=pl.Buffered(1)
            ),
            scratch_shapes=[
                pltpu.VMEM((rows, sum(p.shape[1] for p in pieces)), jnp.bfloat16),
                pltpu.VMEM((3 * PHASES, rows, depth), jnp.bfloat16),
            ],
        ),
        compiler_params=pltpu.CompilerParams(vmem_limit_bytes=36 << 20),
        name="rows",
    )(bases, slots, *pieces)


def correlate_kernel(factor, count, choices, depth, where_ref, rows_ref, limit_ref, *refs):
    pieces = refs[: count * choices]
    out_ref, held, sums, done = refs[-4:]
    step = pl.program_id(0)
    length = PHASES * depth
    width = held.shape[2]

    @pl.when(step == 0)
    def _():
        for choice in range(choices):

            @pl.when(where_ref[3] == choice)
            def _():
                copies = [
                    pltpu.make_async_copy(pieces[count * choice + k], held.at[k], done.at[k])
                    for k in range(count)
                ]
                for copy in copies:
                    copy.start()
                for copy in copies:
                    copy.wait()

        for k in range(count):
            for slot, phases in enumerate(column_blocks()):
                value = None
                for phase in phases:
                    part = held[k, phase * depth : (phase + 1) * depth].astype(jnp.float32)
                    value = part if value is None else value + part
                sums[k, slot * depth : (slot + 1) * depth] = value.astype(jnp.bfloat16)

    block = min(width, 256)
    for k in range(count):
        for first in range(0, width, block):
            spot = first
            if count > 1:
                spot = pl.multiple_of(where_ref[1 + k] * width + first, block)
            limit = limit_ref[:, pl.ds(spot, block)]

            def write(slot, lag, product, spot=spot, limit=limit):
                value = jnp.where(lag < limit, product, 0.0)
                out_ref[slot, :, pl.ds(spot, block)] = value.astype(jnp.bfloat16)

            @pl.when(step < 4)
            def _():
                quad = 3 - step

                def product(row_slot, column_slot, length):
                    start = pl.multiple_of(row_slot * depth, depth)
                    return factor * nn_dot(
                        rows_ref[:, pl.ds(start, length * depth)],
                        sums[
                            k,
                            column_slot * depth : (column_slot + length) * depth,
                            first : first + block,
                        ],
                    )

                shared = [product(PHASES + 2 * quad + half, 0, 4) for half in range(2)]
                for outer, near in ((0, 0), (1, 1)):

                    def inner(kind):
                        index = 3 * outer + kind
                        return product(2 * PHASES + 3 + 5 * index + quad, 4 + 2 * index, 2)

                    middle = inner(1)
                    for half in range(2):
                        slot = 3 - 2 * half - near
                        write(slot, 4 * step + slot, shared[half] + (middle + inner(2 * half)))

            @pl.when(step == 4)
            def _():
                rows = rows_ref[:, :length]
                write(0, LAGS - 1, factor * nn_dot(rows, held[k, :, first : first + block]))


def correlate(rows, pieces, limits, where, factor, buffer):
    choices, count = len(pieces), len(pieces[0])
    depth = rows.shape[1] // ROW_BLOCKS
    length = PHASES * depth
    portion = rows.shape[0]
    columns = limits.shape[1]
    run = pieces[0][0].shape[1]
    across = count * run
    pieces = [piece for group in pieces for piece in group]
    operands = [where, rows, limits, *pieces]
    in_specs = [
        pl.BlockSpec(rows.shape, lambda l, where: (0, 0), pipeline_mode=pl.Buffered(1)),
        pl.BlockSpec((1, across), lambda l, where: (0, where[0])),
    ] + [pl.BlockSpec(memory_space=pl.ANY) for _ in pieces]
    aliases = {}
    if buffer is not None:
        aliases = {len(operands): 0}
        operands.append(buffer)
        in_specs.append(pl.BlockSpec(memory_space=pl.ANY))
    work = LAGS * portion * across
    return pl.pallas_call(
        functools.partial(correlate_kernel, factor, count, choices, depth),
        out_shape=jax.ShapeDtypeStruct((LAGS, portion, columns), jnp.bfloat16),
        grid_spec=pltpu.PrefetchScalarGridSpec(
            num_scalar_prefetch=1,
            grid=(pl.cdiv(LAGS, 4),),
            in_specs=in_specs,
            out_specs=pl.BlockSpec((4, portion, across), lambda l, where: (l, 0, where[0])),
            scratch_shapes=[
                pltpu.VMEM((count, length, run), jnp.bfloat16),
                pltpu.VMEM((count, COLUMN_BLOCKS * depth, run), jnp.bfloat16),
                pltpu.SemaphoreType.DMA((count,)),
            ],
        ),
        input_output_aliases=aliases,
        compiler_params=pltpu.CompilerParams(vmem_limit_bytes=24 << 20),
        cost_estimate=pl.CostEstimate(
            flops=2 * work * length,
            bytes_accessed=2 * (work + rows.size + length * across),
            transcendentals=0,
        ),
        name="correlate",
    )(*operands)


def swap(value, axis):
    return lax.ppermute(value, axis, [(0, 1), (1, 0)])


def shards(recordings, filter_taps, slot_table, lag_count):
    segments, channels, width = recordings.shape
    half = channels // 2
    side = lax.axis_index("sub")
    spot = lax.axis_index("row")
    across = lax.axis_index("col")
    row_count = lax.axis_size("row")
    col_count = lax.axis_size("col")
    portion = slot_table.shape[1] // 2
    factor = 1.0 / math.sqrt(segments * width)

    by_time = recordings.transpose(0, 2, 1)
    away = lax.dynamic_slice_in_dim(by_time, (1 - side) * half, half, 2)
    other = swap(away, "sub")
    mine = whiten(by_time, other, filter_taps, side.reshape(1))

    slots = lax.dynamic_slice_in_dim(slot_table[0], side * portion, portion).reshape(portion, 1)
    limits = lax.dynamic_slice_in_dim(
        lag_count.reshape(row_count, col_count, channels), across, 1, 1
    ).reshape(1, -1)

    if half % 128 or col_count != 2:
        whole = lax.all_gather(mine, "sub", axis=1, tiled=True)
        block = lax.all_gather(whole, "col", axis=1, tiled=True)
        rows = build_rows(slots, [block], jnp.zeros((1,), jnp.int32))
        columns = lax.all_gather(whole, "row", axis=1, tiled=True)
        start = jnp.zeros((4,), jnp.int32)
        result = correlate(rows, [[columns]], limits, start, factor, None)
        return result.reshape(LAGS, portion, 1, -1)

    rightward = [(i, i + 1) for i in range(row_count - 1)]
    leftward = [(i + 1, i) for i in range(row_count - 1)]

    def step(left, right):
        return lax.ppermute(left, "row", rightward), lax.ppermute(right, "row", leftward)

    mate = swap(mine, "sub")
    beside = swap(mine, "col")
    arrived = step(mine, mine)
    beside_mate = swap(beside, "sub")
    near, far = across * channels, (1 - across) * channels
    this, that = side * half, (1 - side) * half
    bases = jnp.stack([near + this, near + that, far + this, far + that]).astype(jnp.int32)
    beside, beside_mate, *arrived = lax.optimization_barrier((beside, beside_mate, *arrived))
    lefts, rights = [mine, arrived[0]], [mine, arrived[1]]
    rows = build_rows(slots, [mine, mate, beside, beside_mate], bases)

    def place(source, choice):
        return jnp.stack([source, side, 1 - side, choice]).astype(jnp.int32)

    orders = []
    for z in range(row_count):
        order = []
        for distance in range(1, row_count):
            ends = [(distance, 1), (distance, -1)]
            order += [(d, sign) for d, sign in ends if 0 <= z + sign * d < row_count]
        orders.append(order)

    mates = {}

    def choose(turn):
        kinds = sorted({orders[z][turn] for z in range(row_count)})
        pieces = []
        for distance, sign in kinds:
            piece = (rights if sign > 0 else lefts)[distance]
            if (distance, sign) not in mates:
                mates[distance, sign] = swap(piece, "sub")
            pieces.append([piece, mates[distance, sign]])
        source = choice = jnp.int32(0)
        for z in range(row_count):
            distance, sign = orders[z][turn]
            source = jnp.where(spot == z, z + sign * distance, source)
            choice = jnp.where(spot == z, kinds.index((distance, sign)), choice)
        return pieces, place(source, choice)

    result = None
    group, where = [[mine, mate]], place(spot, jnp.int32(0))
    for turn in range(row_count):
        last = turn == row_count - 1
        ahead = turn + 2 <= row_count - 1
        if ahead:
            arrived = step(lefts[-1], rights[-1])
        if not last:
            following = choose(turn)
        result = correlate(rows, group, limits, where, factor, result)
        if ahead:
            result, *arrived = lax.optimization_barrier((result, *arrived))
            lefts.append(arrived[0])
            rights.append(arrived[1])
        if not last:
            group, where = following
    return result.reshape(LAGS, portion, 1, -1)


def solution(mesh):
    return jax.shard_map(
        shards,
        mesh=mesh,
        in_specs=(P("grp", ("row", "col"), "sub"), P(), P("row", None), P()),
        out_specs=P("grp", ("row", "sub"), "col", None),
        check_vma=False,
    )
```
